32 devices in a mesh: area: 8 (over z, x), row: 4 (over y, core).
Axes of the slice: x: 2, y: 2, z: 4, core: 2. Of those that a mesh axis runs over, the one named last changes fastest.
Arguments:
- conductance_inverse: float32 [32, 1024, 1024], P(('area', 'row')), as said below
- cap_history: float32 [32, 1024, 128], P(('area', 'row')), may hold values from -3 to 3
- cap_conductance: float32 [32, 1024], P(('area', 'row')), may hold values from 0.5 to 0.8
- wave_history: float32 [32, 40, 32, 128], P(('area', 'row')), may hold values from -6 to 6
- line_partner: int32 [32, 32], P(('area', 'row')), may hold values from 0 to 31, as said below
- line_node: int32 [32, 32], P(('area', 'row')), may hold values from 0 to 1023
- line_delay: int32 [32, 32], P(('area', 'row')), may hold values from 20 to 40
- line_admittance: float32 [32, 32], P(('area', 'row')), may hold values from 0.2 to 1
- conv_node: int32 [32, 64], P(('area', 'row')), may hold values from 0 to 1023
- conv_count: int32 [32], P(('area', 'row')), may hold values from 1 to 64, as said below
- conv_state: float32 [32, 2, 64, 128], P(('area', 'row')), may hold values from -3 to 3
- conv_reference: float32 [32, 2, 64, 128], P(('area', 'row')), may hold values from -4 to 4
- conv_rate: float32 [32, 64], P(('area', 'row')), may hold values from 0.03 to 0.6
- conv_limit: float32 [32, 64], P(('area', 'row')), may hold values from 1 to 2.5
- port_node: int32 [32, 8], P(('area', 'row')), may hold values from 0 to 1023
- port_admittance: float32 [32, 8], P(('area', 'row')), may hold values from 0.3 to 1.2
- port_voltage_prev: float32 [2, 32, 8, 128], P(None, ('area', 'row')), may hold values from -5 to 5
- port_bus: int32 [32, 8], P('area'), may hold values from 0 to 20479
- transfer_impedance: float32 [2, 20480, 256], P(None, 'row', 'area'), may hold values from -0.75 to 0.75
Outputs:
- waves: float32 [32, 20, 32, 128], P(('area', 'row'))
- cap_history_out: float32 [32, 1024, 128], P(('area', 'row'))
- conv_state_out: float32 [32, 2, 64, 128], P(('area', 'row'))
- bus_voltage: float32 [2, 20480, 128], P(None, 'row')
- port_voltage: float32 [2, 32, 8, 128], P(None, ('area', 'row'))
The draws below stay inside these ranges and needn't reach their ends.
Inputs may be any that keep to these rules, and one draw needn't show every extreme that they name: Slot l < 16 of subnetwork s and slot l + 16 of subnetwork (s + k_l) mod 32 are the two ends of one line, with k_l in 1 or 2 the same for every subnetwork and exactly 12 of the k_l equal to 1; so line_partner[s, l] = (s + k_l) mod 32 and line_partner[s, l + 16] = (s - k_l) mod 32. `conv_count`: some subnetwork has all 64 converters in service. `conductance_inverse`: each subnetwork's inverse nodal conductance matrix.
All inputs are finite; a program needn't handle non-finite values.
Results may differ from the reference program's by a relative error of at most 0.0003.
Values sent between devices are 32-bit elements; how exact they have to be, the bound alone decides.
A program may use at most 64 MiB of HBM per device.

```python
import math
import jax
import jax.numpy as jnp
from jax import lax

NODES = 1024
CASES = 128
STEPS = 20
HIST = 40
LINES = 32
NEAR = 12
CONV = 64
PORTS = 8
NB = 20480
SUBNETS = 32
NPORT = 256


def draw_conductance_inverse(key, part):
    first, second = jax.random.split(key)
    diagonal = 0.5 + 0.4 * jax.random.uniform(first, (SUBNETS, NODES), dtype=jnp.float32)
    spread = jax.random.normal(second, (SUBNETS, NODES, NODES), dtype=jnp.float32) * (0.2 / NODES ** 0.5)
    return spread + diagonal[:, :, None] * jnp.eye(NODES, dtype=jnp.float32)[None, :, :]


def draw_line_partner(key, part):
    order = jax.random.permutation(jax.random.fold_in(key, 11), LINES // 2)
    reach = jnp.where(order < NEAR, 1, 2).astype(jnp.int32)
    subnet = jnp.arange(SUBNETS, dtype=jnp.int32)[:, None]
    upper = (subnet + reach[None, :]) % SUBNETS
    lower = (subnet - reach[None, :]) % SUBNETS
    return jnp.concatenate([upper, lower], axis=1).astype(jnp.int32)


def draw_conv_count(key, part):
    first, second = jax.random.split(jax.random.fold_in(key, 23))
    counts = jax.random.randint(first, (SUBNETS,), 1, CONV + 1, dtype=jnp.int32)
    where_full = jax.random.randint(second, (), 0, SUBNETS, dtype=jnp.int32)
    return counts.at[where_full].set(CONV).astype(jnp.int32)


def place_ends(result, rng, least, top_value):
    extent = result.shape
    place = [jax.random.randint(jax.random.fold_in(rng, axis), (), 0, extent[axis]) for axis in range(len(extent))]
    result = result.at[tuple(place)].set(least)
    longest = extent.index(max(extent))
    place[longest] = (place[longest] + 1) % extent[longest]
    return result.at[tuple(place)].set(top_value)


def block_levels(key, extent, pieces, low, top_value):
    def one(dim, parts):
        steps = jax.random.uniform(jax.random.fold_in(jax.random.fold_in(key, 6), dim), (parts,), jnp.float32, low / len(pieces), top_value / len(pieces))
        return jnp.repeat(jnp.exp(steps), extent[dim] // parts).reshape((-1,) + (1,) * (len(extent) - dim - 1))

    gain = one(*pieces[0])
    for cut in pieces[1:]:
        gain = gain * one(*cut)
    return gain


def noise(rng, extent, deviation, most, cuts=(), held_as=jnp.bfloat16):
    values = jax.random.normal(rng, extent, jnp.float32) * deviation
    if len(cuts) > 0:
        values = block_levels(rng, extent, cuts, -0.22, 0.18) * values
    return jnp.clip(values, min=-most, max=most).astype(held_as)


def setup_inputs(seed: int = 0) -> dict:
    streams_of = jax.random.split(jax.random.key(seed), 20)
    return {
        "conductance_inverse": draw_conductance_inverse(jax.random.fold_in(streams_of[19], 71), 0),
        "cap_history": noise(streams_of[1], (SUBNETS, NODES, CASES), 0.5, 3.0, ((0, 32),), jnp.float32),
        "cap_conductance": jnp.clip(0.5 + 0.3 * jax.random.uniform(streams_of[2], (SUBNETS, NODES), jnp.float32) ** block_levels(streams_of[2], (SUBNETS, NODES), ((0, 32),), -0.2, 0.2), 0.5, 0.8),
        "wave_history": noise(streams_of[3], (SUBNETS, HIST, LINES, CASES), 1.0, 6.0, ((0, 32),), jnp.float32),
        "line_partner": draw_line_partner(jax.random.fold_in(streams_of[19], 71), 0),
        "line_node": place_ends(jax.random.randint(streams_of[5], (SUBNETS, LINES), 0, NODES), jax.random.fold_in(streams_of[5], 1), 0, NODES - 1).astype(jnp.int32),
        "line_delay": place_ends(jax.random.randint(streams_of[6], (SUBNETS, LINES), STEPS, 2 * STEPS + 1), jax.random.fold_in(streams_of[6], 1), STEPS, 2 * STEPS).astype(jnp.int32),
        "line_admittance": jnp.clip(0.2 + 0.8 * jax.random.uniform(streams_of[7], (SUBNETS, LINES), jnp.float32) ** block_levels(streams_of[7], (SUBNETS, LINES), ((0, 32),), -0.2, 0.2), 0.2, 1.0),
        "conv_node": place_ends(jax.random.randint(streams_of[8], (SUBNETS, CONV), 0, NODES), jax.random.fold_in(streams_of[8], 1), 0, NODES - 1).astype(jnp.int32),
        "conv_count": draw_conv_count(jax.random.fold_in(streams_of[19], 71), 0),
        "conv_state": noise(streams_of[10], (SUBNETS, 2, CONV, CASES), 0.5, 3.0, ((0, 32),), jnp.float32),
        "conv_reference": noise(streams_of[11], (SUBNETS, 2, CONV, CASES), 1.0, 4.0, ((0, 32),), jnp.float32),
        "conv_rate": jnp.clip(jnp.exp(math.log(0.6) - 2.9957323 * jax.random.uniform(streams_of[12], (SUBNETS, CONV), jnp.float32) ** block_levels(streams_of[12], (SUBNETS, CONV), ((0, 32),), -0.2, 0.2)), 0.03, 0.6),
        "conv_limit": jnp.clip(1.0 + 1.5 * jax.random.uniform(streams_of[13], (SUBNETS, CONV), jnp.float32) ** block_levels(streams_of[13], (SUBNETS, CONV), ((0, 32),), -0.2, 0.2), 1.0, 2.5),
        "port_node": place_ends(jax.random.randint(streams_of[14], (SUBNETS, PORTS), 0, NODES), jax.random.fold_in(streams_of[14], 1), 0, NODES - 1).astype(jnp.int32),
        "port_admittance": jnp.clip(0.3 + 0.90000004 * jax.random.uniform(streams_of[15], (SUBNETS, PORTS), jnp.float32) ** block_levels(streams_of[15], (SUBNETS, PORTS), ((0, 32),), -0.2, 0.2), 0.3, 1.2),
        "port_voltage_prev": noise(streams_of[16], (2, SUBNETS, PORTS, CASES), 1.0, 5.0, ((1, 32),), jnp.float32),
        "port_bus": place_ends(jax.random.randint(streams_of[17], (SUBNETS, PORTS), 0, NB), jax.random.fold_in(streams_of[17], 1), 0, NB - 1).astype(jnp.int32),
        "transfer_impedance": noise(streams_of[18], (2, NB, NPORT), (NPORT // 4) ** -0.5, 0.75, ((1, 4), (2, 8)), jnp.float32),
    }


HIGHEST = lax.Precision.HIGHEST
SAG_FACTOR = 0.3


def window(ginv, start_hist, gcap, incoming, lnode, ladm, cnode, ccount, cstate, setpoint_flow, crate, climit, pnode, padm, pvolt):
    nodes = ginv.shape[0]
    lines = lnode.shape[0]
    convs = cnode.shape[0]
    index = jnp.concatenate([lnode, cnode, pnode]).astype(jnp.int32)
    onehot = (jnp.arange(nodes, dtype=jnp.int32)[:, None] == index[None, :]).astype(jnp.float32)
    picker = onehot.T
    live = (jnp.arange(convs, dtype=jnp.int32) < ccount)[:, None]
    angles = jnp.arange(1, STEPS + 1, dtype=jnp.float32) * jnp.float32(2.0 * math.pi / STEPS)
    limit = climit[:, None]
    slew_limit = crate[:, None]

    def advance(carry, inputs):
        hist_now, inverter_axial_part, inverter_normal_part, acc_re, acc_im = carry
        inward, angle = inputs
        angle_cos_factor = jnp.cos(angle)
        angle_sin_factor = jnp.sin(angle)
        drive = jnp.where(live, inverter_axial_part * angle_cos_factor - inverter_normal_part * angle_sin_factor, 0.0)
        source = padm[:, None] * (pvolt[0] * angle_cos_factor - pvolt[1] * angle_sin_factor)
        stacked = jnp.concatenate([inward, drive, source], axis=0)
        right = hist_now + jnp.dot(onehot, stacked, precision=HIGHEST)
        volt = jnp.dot(ginv, right, precision=HIGHEST)
        probe = jnp.dot(picker, volt, precision=HIGHEST)
        at_line = probe[:lines]
        inverter_emf = probe[lines:lines + convs]
        at_port = probe[lines + convs:]
        outward = 2.0 * ladm[:, None] * at_line - inward
        flow = source - padm[:, None] * at_port
        acc_re = acc_re + flow * angle_cos_factor
        acc_im = acc_im - flow * angle_sin_factor
        unclipped_axial_part = inverter_axial_part + slew_limit * (setpoint_flow[0] - inverter_axial_part) - SAG_FACTOR * inverter_emf * angle_cos_factor
        unclipped_normal_part = inverter_normal_part + slew_limit * (setpoint_flow[1] - inverter_normal_part) + SAG_FACTOR * inverter_emf * angle_sin_factor
        inverter_axial_part = jnp.where(live, limit * jnp.tanh(unclipped_axial_part / limit), inverter_axial_part)
        inverter_normal_part = jnp.where(live, limit * jnp.tanh(unclipped_normal_part / limit), inverter_normal_part)
        hist_now = 2.0 * gcap[:, None] * volt - hist_now
        return (hist_now, inverter_axial_part, inverter_normal_part, acc_re, acc_im), outward

    zeros = jnp.zeros(pvolt.shape[1:], dtype=jnp.float32)
    carry = (start_hist, cstate[0], cstate[1], zeros, zeros)
    carry, outward = lax.scan(advance, carry, (incoming, angles))
    hist_end, inverter_axial_part, inverter_normal_part, acc_re, acc_im = carry
    current = jnp.stack([acc_re, acc_im]) * jnp.float32(2.0 / STEPS)
    return outward, hist_end, jnp.stack([inverter_axial_part, inverter_normal_part]), current


def reference(conductance_inverse, cap_history, cap_conductance, wave_history, line_partner, line_node, line_delay, line_admittance, conv_node, conv_count, conv_state, conv_reference, conv_rate, conv_limit, port_node, port_admittance, port_voltage_prev, port_bus, transfer_impedance):
    remote = (jnp.arange(LINES, dtype=jnp.int32) + LINES // 2) % LINES
    times = jnp.arange(STEPS, dtype=jnp.int32)

    def one_subnet(items):
        ginv, start_hist, gcap, partner, lnode, delay, ladm, cnode, ccount, cstate, setpoint_flow, crate, climit, pnode, padm, pvolt = items
        rows = wave_history[partner, :, remote, :]
        where_now = (times[None, :] - delay[:, None] + HIST).astype(jnp.int32)
        delayed = jnp.take_along_axis(rows, where_now[:, :, None], axis=1)
        incoming = jnp.transpose(delayed, (1, 0, 2))
        return window(ginv, start_hist, gcap, incoming, lnode, ladm, cnode, ccount, cstate, setpoint_flow, crate, climit, pnode, padm, pvolt)

    pvolt_all = jnp.transpose(port_voltage_prev, (1, 0, 2, 3))
    waves, hist_end, conv_out, current = lax.map(one_subnet, (conductance_inverse, cap_history, cap_conductance, line_partner, line_node, line_delay, line_admittance, conv_node, conv_count, conv_state, conv_reference, conv_rate, conv_limit, port_node, port_admittance, pvolt_all))
    flat = jnp.transpose(current, (1, 0, 2, 3)).reshape(2, SUBNETS * PORTS, CASES)
    real = jnp.dot(transfer_impedance[0], flat[0], precision=HIGHEST) - jnp.dot(transfer_impedance[1], flat[1], precision=HIGHEST)
    imag = jnp.dot(transfer_impedance[0], flat[1], precision=HIGHEST) + jnp.dot(transfer_impedance[1], flat[0], precision=HIGHEST)
    bus_voltage = jnp.stack([real, imag])
    port_voltage = bus_voltage[:, port_bus.reshape(-1).astype(jnp.int32), :].reshape(2, SUBNETS, PORTS, CASES)
    return waves, hist_end, conv_out, bus_voltage, port_voltage
```

```python
import functools
import math

import jax
import jax.numpy as jnp
from jax import lax
from jax.experimental import pallas as pl
from jax.experimental.pallas import tpu as pltpu
from jax.sharding import PartitionSpec as P

STEPS = 20
HIST = 40
SAG_FACTOR = 0.3
F32 = jnp.float32
BF16 = jnp.bfloat16


def shifted(x, by):
    axes = ("area", "row")
    size = lax.axis_size(axes)
    return lax.ppermute(x, axes, [(i, (i + by) % size) for i in range(size)])


def split(x):
    high = x.astype(BF16)
    return high, (x - high.astype(F32)).astype(BF16)


def mm(a, b):
    return lax.dot_general(a, b, (((1,), (0,)), ((), ())), preferred_element_type=F32)


def columns(row, count):
    return jnp.broadcast_to(row, (128, count)).T


def window_kernel(
    lines,
    convs,
    ports,
    reach_ref,
    delay_ref,
    trig_ref,
    count_ref,
    index_ref,
    coef_ref,
    ginv_ref,
    gcap_ref,
    hist_ref,
    below1_ref,
    below2_ref,
    above1_ref,
    above2_ref,
    state_ref,
    target_ref,
    pvolt_ref,
    waves_ref,
    hist_out_ref,
    state_out_ref,
    current_ref,
    big,
    wj,
    wx,
    cap2,
    xs,
):
    nodes = ginv_ref.shape[0]
    probes = 128
    half = lines // 2
    rows = 256

    index = columns(index_ref[...].astype(F32), probes).astype(jnp.int32)
    for c in range(nodes // 128):
        lane = lax.broadcasted_iota(jnp.int32, (probes, 128), 1) + 128 * c
        cap2[:, c * 128 : (c + 1) * 128] = jnp.where(index == lane, 1.0, 0.0)
    pick = cap2[...].astype(BF16)
    scatter = cap2[...].T.astype(BF16)
    for r in range(nodes // rows):
        span = pl.ds(r * rows, rows)
        high, low = split(ginv_ref[span, :])
        big[span, 0:nodes] = high
        big[span, nodes : 2 * nodes] = low
    tail = pl.ds(nodes, probes)
    big[tail, :nodes] = mm(pick, big[0:nodes, 0:nodes]).astype(BF16)
    big[tail, nodes : 2 * nodes] = mm(pick, big[0:nodes, nodes : 2 * nodes]).astype(BF16)
    big[:, 2 * nodes : 2 * nodes + 128] = mm(big[:, 0:nodes], scatter).astype(BF16)
    big[:, 2 * nodes + 128 :] = mm(big[:, nodes : 2 * nodes], scatter).astype(BF16)
    gcap = 2.0 * columns(gcap_ref[...], nodes)

    def put_state(value):
        high, low = split(value)
        wj[:, 0:128] = high
        wj[:, 128:256] = low

    hist_out_ref[...] = hist_ref[...]
    put_state(hist_ref[...])
    state_out_ref[...] = state_ref[...]
    current_ref[...] = jnp.zeros_like(current_ref)
    coef = coef_ref[...]
    two_adm = columns(coef[0:1], 128)[0:lines]
    rate = columns(coef[1:2], 128)[lines : lines + convs]
    limit = columns(coef[2:3], 128)[lines : lines + convs]
    padm = columns(coef[0:1], 128)[lines + convs : lines + convs + ports]
    live = lax.broadcasted_iota(jnp.int32, (convs, 128), 0) < count_ref[0]
    xs[lines + convs + ports :, :] = jnp.zeros((probes - lines - convs - ports, 128), F32)

    def step(t, carry):
        cosine = trig_ref[0, t]
        sine = trig_ref[1, t]
        for l in range(half):
            up = t - delay_ref[l] + HIST
            down = t - delay_ref[l + half] + HIST
            near = reach_ref[l] == 1
            xs[l : l + 1, :] = jnp.where(near, above1_ref[up, l : l + 1, :], above2_ref[up, l : l + 1, :])
            xs[l + half : l + half + 1, :] = jnp.where(
                near, below1_ref[down, l : l + 1, :], below2_ref[down, l : l + 1, :]
            )
        inward = xs[0:lines, :]
        axial = state_out_ref[0]
        normal = state_out_ref[1]
        source = padm * (pvolt_ref[0] * cosine - pvolt_ref[1] * sine)
        xs[lines : lines + convs, :] = jnp.where(live, axial * cosine - normal * sine, 0.0)
        xs[lines + convs : lines + convs + ports, :] = source
        high, low = split(xs[...])
        wx[0:128, 0:128] = high
        wx[128:256, 0:128] = high
        wx[0:128, 128:256] = low
        wx[128:256, 128:256] = low

        def apply(start, size):
            span = pl.ds(start, size)
            both = (
                mm(big[span, 0:nodes], wj[...])
                + mm(big[span, nodes : 2 * nodes], wj[...])
                + mm(big[span, 2 * nodes :], wx[...])
            )
            return both[:, 0:128] + both[:, 128:256]

        probe = apply(nodes, probes)
        volts = apply(0, nodes)
        waves_ref[t] = two_adm * probe[0:lines] - inward
        emf = probe[lines : lines + convs]
        flow = source - padm * probe[lines + convs : lines + convs + ports]
        current_ref[0] += flow * cosine
        current_ref[1] -= flow * sine
        new_axial = axial + rate * (target_ref[0] - axial) - SAG_FACTOR * emf * cosine
        new_normal = normal + rate * (target_ref[1] - normal) + SAG_FACTOR * emf * sine
        state_out_ref[0] = jnp.where(live, limit * jnp.tanh(new_axial / limit), axial)
        state_out_ref[1] = jnp.where(live, limit * jnp.tanh(new_normal / limit), normal)
        after = gcap * volts - hist_out_ref[...]
        hist_out_ref[...] = after
        put_state(after)
        return carry

    lax.fori_loop(0, STEPS, step, 0)
    current_ref[...] = current_ref[...] * (2.0 / STEPS)


def bus_kernel(zt_ref, currents_ref, out_ref, rh, rl):
    @pl.when(pl.program_id(0) == 0)
    def _():
        high, low = split(currents_ref[...])
        rh[...] = high
        rl[...] = low

    zt = zt_ref[...].T
    high, low = split(zt)
    total = mm(high, rh[...]) + mm(low, rh[...]) + mm(high, rl[...])
    out_ref[0] = total[:, 0:128]
    out_ref[1] = total[:, 128:256]


def vmem():
    return pl.BlockSpec(memory_space=pltpu.VMEM)


def smem():
    return pl.BlockSpec(memory_space=pltpu.SMEM)


def per_device(
    conductance_inverse,
    cap_history,
    cap_conductance,
    wave_history,
    line_partner,
    line_node,
    line_delay,
    line_admittance,
    conv_node,
    conv_count,
    conv_state,
    conv_reference,
    conv_rate,
    conv_limit,
    port_node,
    port_admittance,
    port_voltage_prev,
    port_bus,
    transfer_impedance,
):
    subnets = lax.axis_size(("area", "row"))
    own = lax.axis_index(("area", "row"))
    history = wave_history[0]
    lines = history.shape[1]
    half = lines // 2
    cases = history.shape[2]
    nodes = conductance_inverse.shape[1]
    convs = conv_node.shape[1]
    ports = port_node.shape[1]
    upper = history[:, :half]
    lower = history[:, half:]
    below1 = shifted(upper, 1)
    above1 = shifted(lower, -1)
    below2 = shifted(upper, 2)
    above2 = shifted(lower, -2)
    reach = (line_partner[0] - own) % subnets
    zt = jnp.transpose(transfer_impedance, (0, 2, 1))
    zt_all = lax.all_gather(zt, "area", axis=0, tiled=False)

    pad = 128 - lines - convs - ports
    index = jnp.concatenate([line_node, conv_node, port_node, jnp.full((1, pad), -1, jnp.int32)], axis=1)
    ones = jnp.ones((1, 128 - lines - convs), F32)
    coef = jnp.concatenate(
        [
            jnp.concatenate([2.0 * line_admittance, jnp.ones((1, convs), F32), port_admittance, ones[:, :pad]], axis=1),
            jnp.concatenate([jnp.ones((1, lines), F32), conv_rate, ones], axis=1),
            jnp.concatenate([jnp.ones((1, lines), F32), conv_limit, ones], axis=1),
        ],
        axis=0,
    )
    angles = jnp.arange(1, STEPS + 1, dtype=F32) * jnp.float32(2.0 * math.pi / STEPS)
    trig = jnp.stack([jnp.cos(angles), jnp.sin(angles)])
    flops = 2 * STEPS * (nodes + 128) * (2 * nodes + 256) * 256
    waves, hist_end, conv_out, current = pl.pallas_call(
        functools.partial(window_kernel, lines, convs, ports),
        out_shape=(
            jax.ShapeDtypeStruct((STEPS, lines, cases), F32),
            jax.ShapeDtypeStruct((nodes, cases), F32),
            jax.ShapeDtypeStruct((2, convs, cases), F32),
            jax.ShapeDtypeStruct((2, ports, cases), F32),
        ),
        in_specs=[smem()] * 4 + [vmem()] * 12,
        out_specs=(vmem(),) * 4,
        scratch_shapes=[
            pltpu.VMEM((nodes + 128, 2 * nodes + 256), BF16),
            pltpu.VMEM((nodes, 256), BF16),
            pltpu.VMEM((256, 256), BF16),
            pltpu.VMEM((128, nodes), F32),
            pltpu.VMEM((128, 128), F32),
        ],
        cost_estimate=pl.CostEstimate(flops=flops, bytes_accessed=8_000_000, transcendentals=0),
        name="window",
    )(
        reach,
        line_delay[0],
        trig,
        conv_count,
        index,
        coef,
        conductance_inverse[0],
        cap_conductance,
        cap_history[0],
        below1,
        below2,
        above1,
        above2,
        conv_state[0],
        conv_reference[0],
        port_voltage_prev[:, 0],
    )

    areas = lax.axis_size("area")
    rows = lax.axis_size("row")
    bus_rows = transfer_impedance.shape[1]
    members = transfer_impedance.shape[2]
    piece = lax.all_gather(current, ("area", "row"), axis=0, tiled=False)
    piece = piece.reshape(areas, rows, 2, ports, cases).transpose(2, 0, 1, 3, 4).reshape(2, areas, members, cases)
    into_re = jnp.concatenate([piece[0], piece[1]], axis=-1)
    into_im = jnp.concatenate([-piece[1], piece[0]], axis=-1)
    flat = jnp.stack([into_re, into_im], axis=1).reshape(areas * 2 * members, 2 * cases)
    depth = flat.shape[0]
    block = 512
    bus_voltage = pl.pallas_call(
        bus_kernel,
        grid=(bus_rows // block,),
        out_shape=jax.ShapeDtypeStruct((2, bus_rows, cases), F32),
        in_specs=[
            pl.BlockSpec((depth, block), lambda i: (0, i)),
            pl.BlockSpec((depth, 2 * cases), lambda i: (0, 0)),
        ],
        out_specs=pl.BlockSpec((2, block, cases), lambda i: (0, i, 0)),
        scratch_shapes=[pltpu.VMEM((depth, 2 * cases), BF16)] * 2,
        name="buses",
    )(zt_all.reshape(depth, bus_rows), flat)

    local = port_bus.reshape(-1) - lax.axis_index("row") * bus_rows
    inside = (local >= 0) & (local < bus_rows)
    taken = jnp.take(bus_voltage, jnp.clip(local, 0, bus_rows - 1), axis=1)
    taken = jnp.where(inside[None, :, None], taken, 0.0)
    taken = taken.reshape(2, port_bus.shape[0], port_bus.shape[1], cases)
    port_voltage = lax.psum_scatter(taken, "row", scatter_dimension=1, tiled=True)
    return (waves[None], hist_end[None], conv_out[None], bus_voltage, port_voltage)


def solution(mesh):
    both = ("area", "row")
    placed = (
        P(both, None, None),
        P(both, None, None),
        P(both, None),
        P(both, None, None, None),
        P(both, None),
        P(both, None),
        P(both, None),
        P(both, None),
        P(both, None),
        P(both),
        P(both, None, None, None),
        P(both, None, None, None),
        P(both, None),
        P(both, None),
        P(both, None),
        P(both, None),
        P(None, both, None, None),
        P("area", None),
        P(None, "row", "area"),
    )
    return jax.shard_map(
        per_device,
        mesh=mesh,
        in_specs=placed,
        out_specs=(
            P(both, None, None, None),
            P(both, None, None),
            P(both, None, None, None),
            P(None, "row", None),
            P(None, both, None, None),
        ),
        check_vma=False,
    )
```

```python
import functools
import math

import jax
import jax.numpy as jnp
from jax import lax
from jax.experimental import pallas as pl
from jax.experimental.pallas import tpu as pltpu
from jax.sharding import PartitionSpec as P

STEPS = 20
HIST = 40
SAG_FACTOR = 0.3
F32 = jnp.float32
BF16 = jnp.bfloat16
MESH = pl.DeviceIdType.MESH


def shifted(x, by):
    axes = ("area", "row")
    size = lax.axis_size(axes)
    return lax.ppermute(x, axes, [(i, (i + by) % size) for i in range(size)])


def split(x):
    high = x.astype(BF16)
    return high, (x - high.astype(F32)).astype(BF16)


def mm(a, b):
    return lax.dot_general(a, b, (((1,), (0,)), ((), ())), preferred_element_type=F32)


def columns(row, count):
    return jnp.broadcast_to(row, (128, count)).T


def window_kernel(
    lines,
    convs,
    ports,
    reach_ref,
    delay_ref,
    trig_ref,
    count_ref,
    index_ref,
    coef_ref,
    ginv_ref,
    gcap_ref,
    hist_ref,
    below1_ref,
    below2_ref,
    above1_ref,
    above2_ref,
    state_ref,
    target_ref,
    pvolt_ref,
    zc_ref,
    waves_ref,
    hist_out_ref,
    state_out_ref,
    flat_ref,
    bus_ref,
    big,
    wj,
    wx,
    cap2,
    xs,
    current_ref,
    zin,
    cin,
    mine,
    rh,
    rl,
    zs,
    zr,
    rs,
    rr,
    cs,
    cr,
    zlocal,
    os,
    orr,
    fs,
    fr,
    olocal,
):
    nodes = ginv_ref.shape[0]
    probes = 128
    half = lines // 2
    rows = 256
    areas, group = cin.shape[0], cin.shape[1]
    depth, chunk = zin.shape[1], zin.shape[2]
    a = lax.axis_index("area")
    r = lax.axis_index("row")

    barrier = pltpu.get_barrier_semaphore()
    for d in range(1, areas):
        pl.semaphore_signal(barrier, inc=1, device_id=(lax.rem(a + d, areas), r), device_id_type=MESH)
    for d in range(1, group):
        pl.semaphore_signal(barrier, inc=1, device_id=(a, lax.rem(r + d, group)), device_id_type=MESH)
    pl.semaphore_wait(barrier, areas + group - 2)

    def send(src, dst, ssem, rsem, to):
        return pltpu.make_async_remote_copy(
            src_ref=src, dst_ref=dst, send_sem=ssem, recv_sem=rsem, device_id=to, device_id_type=MESH
        )

    own_z = pltpu.make_async_copy(zc_ref.at[a], zin.at[a], zlocal)
    own_z.start()
    z_copies = []
    for d in range(1, areas):
        to = lax.rem(a + d, areas)
        copy = send(zc_ref.at[to], zin.at[a], zs.at[d], zr.at[d], (to, r))
        copy.start()
        z_copies.append(copy)

    index = columns(index_ref[...].astype(F32), probes).astype(jnp.int32)
    for c in range(nodes // 128):
        lane = lax.broadcasted_iota(jnp.int32, (probes, 128), 1) + 128 * c
        cap2[:, c * 128 : (c + 1) * 128] = jnp.where(index == lane, 1.0, 0.0)
    pick = cap2[...].astype(BF16)
    scatter = cap2[...].T.astype(BF16)
    for b in range(nodes // rows):
        span = pl.ds(b * rows, rows)
        high, low = split(ginv_ref[span, :])
        big[span, 0:nodes] = high
        big[span, nodes : 2 * nodes] = low
    tail = pl.ds(nodes, probes)
    big[tail, :nodes] = mm(pick, big[0:nodes, 0:nodes]).astype(BF16)
    big[tail, nodes : 2 * nodes] = mm(pick, big[0:nodes, nodes : 2 * nodes]).astype(BF16)
    big[:, 2 * nodes : 2 * nodes + 128] = mm(big[:, 0:nodes], scatter).astype(BF16)
    big[:, 2 * nodes + 128 :] = mm(big[:, nodes : 2 * nodes], scatter).astype(BF16)
    gcap = 2.0 * columns(gcap_ref[...], nodes)

    def put_state(value):
        high, low = split(value)
        wj[:, 0:128] = high
        wj[:, 128:256] = low

    hist_out_ref[...] = hist_ref[...]
    put_state(hist_ref[...])
    state_out_ref[...] = state_ref[...]
    current_ref[...] = jnp.zeros_like(current_ref)
    coef = coef_ref[...]
    two_adm = columns(coef[0:1], 128)[0:lines]
    rate = columns(coef[1:2], 128)[lines : lines + convs]
    limit = columns(coef[2:3], 128)[lines : lines + convs]
    padm = columns(coef[0:1], 128)[lines + convs : lines + convs + ports]
    live = lax.broadcasted_iota(jnp.int32, (convs, 128), 0) < count_ref[0]
    xs[lines + convs + ports :, :] = jnp.zeros((probes - lines - convs - ports, 128), F32)

    def step(t, carry):
        cosine = trig_ref[0, t]
        sine = trig_ref[1, t]
        for l in range(half):
            up = jnp.clip(t - delay_ref[l] + HIST, 0, HIST - 1)
            down = jnp.clip(t - delay_ref[l + half] + HIST, 0, HIST - 1)
            near = reach_ref[l] == 1
            xs[l : l + 1, :] = jnp.where(near, above1_ref[up, l : l + 1, :], above2_ref[up, l : l + 1, :])
            xs[l + half : l + half + 1, :] = jnp.where(
                near, below1_ref[down, l : l + 1, :], below2_ref[down, l : l + 1, :]
            )
        inward = xs[0:lines, :]
        axial = state_out_ref[0]
        normal = state_out_ref[1]
        source = padm * (pvolt_ref[0] * cosine - pvolt_ref[1] * sine)
        xs[lines : lines + convs, :] = jnp.where(live, axial * cosine - normal * sine, 0.0)
        xs[lines + convs : lines + convs + ports, :] = source
        high, low = split(xs[...])
        wx[0:128, 0:128] = high
        wx[128:256, 0:128] = high
        wx[0:128, 128:256] = low
        wx[128:256, 128:256] = low

        def apply(start, size):
            span = pl.ds(start, size)
            both = (
                mm(big[span, 0:nodes], wj[...])
                + mm(big[span, nodes : 2 * nodes], wj[...])
                + mm(big[span, 2 * nodes :], wx[...])
            )
            return both[:, 0:128] + both[:, 128:256]

        probe = apply(nodes, probes)
        volts = apply(0, nodes)
        waves_ref[t] = two_adm * probe[0:lines] - inward
        emf = probe[lines : lines + convs]
        flow = source - padm * probe[lines + convs : lines + convs + ports]
        current_ref[0] += flow * cosine
        current_ref[1] -= flow * sine
        new_axial = axial + rate * (target_ref[0] - axial) - SAG_FACTOR * emf * cosine
        new_normal = normal + rate * (target_ref[1] - normal) + SAG_FACTOR * emf * sine
        state_out_ref[0] = jnp.where(live, limit * jnp.tanh(new_axial / limit), axial)
        state_out_ref[1] = jnp.where(live, limit * jnp.tanh(new_normal / limit), normal)
        after = gcap * volts - hist_out_ref[...]
        hist_out_ref[...] = after
        put_state(after)
        return carry

    lax.fori_loop(0, STEPS, step, 0)
    cin[a, r] = current_ref[...] * (2.0 / STEPS)

    copies = []
    for d in range(1, group):
        block = cin.at[a, r]
        copy = send(block, block, rs.at[d], rr.at[d], (a, lax.rem(r + d, group)))
        copy.start()
        copies.append(copy)
    for copy in copies:
        copy.wait()
    copies = []
    for d in range(1, areas):
        block = cin.at[a]
        copy = send(block, block, cs.at[d], cr.at[d], (lax.rem(a + d, areas), r))
        copy.start()
        copies.append(copy)
    own_z.wait()
    for copy in z_copies:
        copy.wait()
    for copy in copies:
        copy.wait()
    members = group * ports
    for i in range(areas):
        for j in range(group):
            re, im = cin[i, j, 0], cin[i, j, 1]
            top = i * depth + j * ports
            flat_ref[top : top + ports, 0:128] = re
            flat_ref[top : top + ports, 128:256] = im
            flat_ref[top + members : top + members + ports, 0:128] = -im
            flat_ref[top + members : top + members + ports, 128:256] = re
    high, low = split(flat_ref[...])
    rh[...] = high
    rl[...] = low
    high, low = split(zin[...].reshape(areas * depth, chunk).T)
    total = mm(high, rh[...]) + mm(low, rh[...]) + mm(high, rl[...])
    mine[0] = total[:, 0:128]
    mine[1] = total[:, 128:256]

    inner = 2 ** ((areas.bit_length() - 1) // 2)
    outer = areas // inner
    zi = lax.div(a, inner)
    xi = lax.rem(a, inner)

    def region(part, who):
        return bus_ref.at[part, pl.ds(pl.multiple_of(who * chunk, 8), chunk), :]

    pending = []
    arrivals = []
    for part in range(2):
        local = pltpu.make_async_copy(mine.at[part], region(part, a), olocal.at[part])
        local.start()
        pending.append(local)
        for d in range(1, inner):
            to = zi * inner + lax.rem(xi + d, inner)
            k = part * areas + d
            copy = send(mine.at[part], region(part, a), os.at[k], orr.at[k], (to, r))
            copy.start()
            pending.append(copy)
        for d in range(1, outer):
            to = lax.rem(zi + d, outer) * inner + xi
            k = part * areas + inner * d
            copy = send(mine.at[part], region(part, a), os.at[k], orr.at[k], (to, r))
            copy.start()
            arrivals.append((part, d, copy))
    for part, d, copy in arrivals:
        copy.wait_recv()
        source = lax.rem(zi + outer - d, outer) * inner + xi
        for e in range(1, inner):
            to = zi * inner + lax.rem(xi + e, inner)
            k = part * areas + inner * d + e
            block = region(part, source)
            forward = send(block, block, fs.at[k], fr.at[k], (to, r))
            forward.start()
            pending.append(forward)
    for _, _, copy in arrivals:
        copy.wait_send()
    for copy in pending:
        copy.wait()


def vmem():
    return pl.BlockSpec(memory_space=pltpu.VMEM)


def smem():
    return pl.BlockSpec(memory_space=pltpu.SMEM)


def per_device(
    conductance_inverse,
    cap_history,
    cap_conductance,
    wave_history,
    line_partner,
    line_node,
    line_delay,
    line_admittance,
    conv_node,
    conv_count,
    conv_state,
    conv_reference,
    conv_rate,
    conv_limit,
    port_node,
    port_admittance,
    port_voltage_prev,
    port_bus,
    transfer_impedance,
):
    subnets = lax.axis_size(("area", "row"))
    own = lax.axis_index(("area", "row"))
    history = wave_history[0]
    lines = history.shape[1]
    half = lines // 2
    cases = history.shape[2]
    nodes = conductance_inverse.shape[1]
    convs = conv_node.shape[1]
    ports = port_node.shape[1]
    upper = history[:, :half]
    lower = history[:, half:]
    below1 = shifted(upper, 1)
    above1 = shifted(lower, -1)
    below2 = shifted(upper, 2)
    above2 = shifted(lower, -2)
    reach = (line_partner[0] - own) % subnets
    areas = lax.axis_size("area")
    group = lax.axis_size("row")
    bus_rows = transfer_impedance.shape[1]
    members = transfer_impedance.shape[2]
    chunk = bus_rows // areas
    zt = jnp.transpose(transfer_impedance, (0, 2, 1)).reshape(2 * members, bus_rows)
    zc = jnp.transpose(zt.reshape(2 * members, areas, chunk), (1, 0, 2))
    all_bus = lax.all_gather(port_bus, "area", axis=0, tiled=False).reshape(-1)
    local = all_bus - lax.axis_index("row") * bus_rows
    pick = (jnp.arange(bus_rows, dtype=jnp.int32)[:, None] == local[None, :]).astype(F32)
    picked = jnp.dot(zt, pick, precision=lax.Precision.HIGHEST).reshape(2 * members, areas, group, ports)
    picked = lax.psum_scatter(picked, "row", scatter_dimension=2, tiled=True).reshape(2 * members, areas * ports)
    picked = lax.all_gather(picked, "area", axis=0, tiled=True)
    zport = lax.dynamic_slice_in_dim(picked, lax.axis_index("area") * ports, ports, 1)

    pad = 128 - lines - convs - ports
    index = jnp.concatenate([line_node, conv_node, port_node, jnp.full((1, pad), -1, jnp.int32)], axis=1)
    ones = jnp.ones((1, 128 - lines - convs), F32)
    coef = jnp.concatenate(
        [
            jnp.concatenate([2.0 * line_admittance, jnp.ones((1, convs), F32), port_admittance, ones[:, :pad]], axis=1),
            jnp.concatenate([jnp.ones((1, lines), F32), conv_rate, ones], axis=1),
            jnp.concatenate([jnp.ones((1, lines), F32), conv_limit, ones], axis=1),
        ],
        axis=0,
    )
    angles = jnp.arange(1, STEPS + 1, dtype=F32) * jnp.float32(2.0 * math.pi / STEPS)
    trig = jnp.stack([jnp.cos(angles), jnp.sin(angles)])
    flops = 2 * STEPS * (nodes + 128) * (2 * nodes + 256) * 256
    waves, hist_end, conv_out, flat, bus_voltage = pl.pallas_call(
        functools.partial(window_kernel, lines, convs, ports),
        out_shape=(
            jax.ShapeDtypeStruct((STEPS, lines, cases), F32),
            jax.ShapeDtypeStruct((nodes, cases), F32),
            jax.ShapeDtypeStruct((2, convs, cases), F32),
            jax.ShapeDtypeStruct((areas * 2 * members, 2 * cases), F32),
            jax.ShapeDtypeStruct((2, bus_rows, cases), F32),
        ),
        in_specs=[smem()] * 4 + [vmem()] * 12 + [pl.BlockSpec(memory_space=pl.ANY)],
        out_specs=(vmem(),) * 4 + (pl.BlockSpec(memory_space=pl.ANY),),
        scratch_shapes=[
            pltpu.VMEM((nodes + 128, 2 * nodes + 256), BF16),
            pltpu.VMEM((nodes, 256), BF16),
            pltpu.VMEM((256, 256), BF16),
            pltpu.VMEM((128, nodes), F32),
            pltpu.VMEM((128, 128), F32),
            pltpu.VMEM((2, ports, cases), F32),
            pltpu.VMEM((areas, 2 * members, chunk), F32),
            pltpu.VMEM((areas, group, 2, ports, cases), F32),
            pltpu.VMEM((2, chunk, cases), F32),
            pltpu.VMEM((areas * 2 * members, 2 * cases), BF16),
            pltpu.VMEM((areas * 2 * members, 2 * cases), BF16),
            pltpu.SemaphoreType.DMA((areas,)),
            pltpu.SemaphoreType.DMA((areas,)),
            pltpu.SemaphoreType.DMA((group,)),
            pltpu.SemaphoreType.DMA((group,)),
            pltpu.SemaphoreType.DMA((areas,)),
            pltpu.SemaphoreType.DMA((areas,)),
            pltpu.SemaphoreType.DMA,
            pltpu.SemaphoreType.DMA((2 * areas,)),
            pltpu.SemaphoreType.DMA((2 * areas,)),
            pltpu.SemaphoreType.DMA((2 * areas,)),
            pltpu.SemaphoreType.DMA((2 * areas,)),
            pltpu.SemaphoreType.DMA((2,)),
        ],
        compiler_params=pltpu.CompilerParams(collective_id=0, has_side_effects=True),
        cost_estimate=pl.CostEstimate(flops=flops, bytes_accessed=8_000_000, transcendentals=0),
        name="window",
    )(
        reach,
        line_delay[0],
        trig,
        conv_count,
        index,
        coef,
        conductance_inverse[0],
        cap_conductance,
        cap_history[0],
        below1,
        below2,
        above1,
        above2,
        conv_state[0],
        conv_reference[0],
        port_voltage_prev[:, 0],
        zc,
    )

    seen = lax.dot_general(zport, flat, (((0,), (0,)), ((), ())), precision=lax.Precision.HIGHEST)
    port_voltage = jnp.stack([seen[:, :cases], seen[:, cases:]])[:, None]
    return (waves[None], hist_end[None], conv_out[None], bus_voltage, port_voltage)


def solution(mesh):
    both = ("area", "row")
    placed = (
        P(both, None, None),
        P(both, None, None),
        P(both, None),
        P(both, None, None, None),
        P(both, None),
        P(both, None),
        P(both, None),
        P(both, None),
        P(both, None),
        P(both),
        P(both, None, None, None),
        P(both, None, None, None),
        P(both, None),
        P(both, None),
        P(both, None),
        P(both, None),
        P(None, both, None, None),
        P("area", None),
        P(None, "row", "area"),
    )
    return jax.shard_map(
        per_device,
        mesh=mesh,
        in_specs=placed,
        out_specs=(
            P(both, None, None, None),
            P(both, None, None),
            P(both, None, None, None),
            P(None, "row", None),
            P(None, both, None, None),
        ),
        check_vma=False,
    )
```

```python
import functools
import math

import jax
import jax.numpy as jnp
from jax import lax
from jax.experimental import pallas as pl
from jax.experimental.pallas import tpu as pltpu
from jax.sharding import PartitionSpec as P

STEPS = 20
HIST = 40
SAG_FACTOR = 0.3
F32 = jnp.float32
BF16 = jnp.bfloat16
MESH = pl.DeviceIdType.MESH


def shifted(x, by):
    axes = ("area", "row")
    size = lax.axis_size(axes)
    return lax.ppermute(x, axes, [(i, (i + by) % size) for i in range(size)])


def split(x):
    high = x.astype(BF16)
    return high, (x - high.astype(F32)).astype(BF16)


def mm(a, b):
    return lax.dot_general(a, b, (((1,), (0,)), ((), ())), preferred_element_type=F32)


def columns(row, count):
    return jnp.broadcast_to(row, (128, count)).T


def window_kernel(
    lines,
    convs,
    ports,
    reach_ref,
    delay_ref,
    trig_ref,
    count_ref,
    index_ref,
    coef_ref,
    ginv_ref,
    gcap_ref,
    hist_ref,
    below1_ref,
    below2_ref,
    above1_ref,
    above2_ref,
    state_ref,
    target_ref,
    pvolt_ref,
    zc_ref,
    waves_ref,
    hist_out_ref,
    state_out_ref,
    flat_ref,
    bus_ref,
    big,
    wj,
    wx,
    cap2,
    xs,
    current_ref,
    zin,
    cin,
    mine,
    rh,
    rl,
    zs,
    zr,
    rs,
    rr,
    cs,
    cr,
    zlocal,
    os,
    orr,
    fs,
    fr,
    olocal,
):
    nodes = ginv_ref.shape[0]
    probes = 128
    half = lines // 2
    rows = 256
    areas, group = cin.shape[0], cin.shape[1]
    depth, chunk = zin.shape[1], zin.shape[2]
    a = lax.axis_index("area")
    r = lax.axis_index("row")

    barrier = pltpu.get_barrier_semaphore()
    for d in range(1, areas):
        pl.semaphore_signal(barrier, inc=1, device_id=(lax.rem(a + d, areas), r), device_id_type=MESH)
    for d in range(1, group):
        pl.semaphore_signal(barrier, inc=1, device_id=(a, lax.rem(r + d, group)), device_id_type=MESH)
    pl.semaphore_wait(barrier, areas + group - 2)

    def send(src, dst, ssem, rsem, to):
        return pltpu.make_async_remote_copy(
            src_ref=src, dst_ref=dst, send_sem=ssem, recv_sem=rsem, device_id=to, device_id_type=MESH
        )

    own_z = pltpu.make_async_copy(zc_ref.at[a], zin.at[a], zlocal)
    own_z.start()
    z_copies = []
    for d in range(1, areas):
        to = lax.rem(a + d, areas)
        copy = send(zc_ref.at[to], zin.at[a], zs.at[d], zr.at[d], (to, r))
        copy.start()
        z_copies.append(copy)

    index = columns(index_ref[...].astype(F32), probes).astype(jnp.int32)
    for c in range(nodes // 128):
        lane = lax.broadcasted_iota(jnp.int32, (probes, 128), 1) + 128 * c
        cap2[:, c * 128 : (c + 1) * 128] = jnp.where(index == lane, 1.0, 0.0)
    pick = cap2[...].astype(BF16)
    scatter = cap2[...].T.astype(BF16)
    for b in range(nodes // rows):
        span = pl.ds(b * rows, rows)
        high, low = split(ginv_ref[span, :])
        big[span, 0:nodes] = high
        big[span, nodes : 2 * nodes] = low
    tail = pl.ds(nodes, probes)
    big[tail, :nodes] = mm(pick, big[0:nodes, 0:nodes]).astype(BF16)
    big[tail, nodes : 2 * nodes] = mm(pick, big[0:nodes, nodes : 2 * nodes]).astype(BF16)
    big[:, 2 * nodes : 2 * nodes + 128] = mm(big[:, 0:nodes], scatter).astype(BF16)
    big[:, 2 * nodes + 128 :] = mm(big[:, nodes : 2 * nodes], scatter).astype(BF16)
    gcap = 2.0 * columns(gcap_ref[...], nodes)

    def put_state(value):
        high, low = split(value)
        wj[:, 0:128] = high
        wj[:, 128:256] = low

    hist_out_ref[...] = hist_ref[...]
    put_state(hist_ref[...])
    state_out_ref[...] = state_ref[...]
    current_ref[...] = jnp.zeros_like(current_ref)
    coef = coef_ref[...]
    two_adm = columns(coef[0:1], 128)[0:lines]
    rate = columns(coef[1:2], 128)[lines : lines + convs]
    limit = columns(coef[2:3], 128)[lines : lines + convs]
    padm = columns(coef[0:1], 128)[lines + convs : lines + convs + ports]
    live = lax.broadcasted_iota(jnp.int32, (convs, 128), 0) < count_ref[0]
    xs[lines + convs + ports :, :] = jnp.zeros((probes - lines - convs - ports, 128), F32)

    def step(t, carry):
        cosine = trig_ref[0, t]
        sine = trig_ref[1, t]
        for l in range(half):
            up = jnp.clip(t - delay_ref[l] + HIST, 0, HIST - 1)
            down = jnp.clip(t - delay_ref[l + half] + HIST, 0, HIST - 1)
            near = reach_ref[l] == 1
            xs[l : l + 1, :] = jnp.where(near, above1_ref[up, l : l + 1, :], above2_ref[up, l : l + 1, :])
            xs[l + half : l + half + 1, :] = jnp.where(
                near, below1_ref[down, l : l + 1, :], below2_ref[down, l : l + 1, :]
            )
        inward = xs[0:lines, :]
        axial = state_out_ref[0]
        normal = state_out_ref[1]
        source = padm * (pvolt_ref[0] * cosine - pvolt_ref[1] * sine)
        xs[lines : lines + convs, :] = jnp.where(live, axial * cosine - normal * sine, 0.0)
        xs[lines + convs : lines + convs + ports, :] = source
        high, low = split(xs[...])
        wx[0:128, 0:128] = high
        wx[128:256, 0:128] = high
        wx[0:128, 128:256] = low
        wx[128:256, 128:256] = low

        def apply(start, size):
            span = pl.ds(start, size)
            both = (
                mm(big[span, 0:nodes], wj[...])
                + mm(big[span, nodes : 2 * nodes], wj[...])
                + mm(big[span, 2 * nodes :], wx[...])
            )
            return both[:, 0:128] + both[:, 128:256]

        probe = apply(nodes, probes)
        volts = apply(0, nodes)
        waves_ref[t] = two_adm * probe[0:lines] - inward
        emf = probe[lines : lines + convs]
        flow = source - padm * probe[lines + convs : lines + convs + ports]
        current_ref[0] += flow * cosine
        current_ref[1] -= flow * sine
        new_axial = axial + rate * (target_ref[0] - axial) - SAG_FACTOR * emf * cosine
        new_normal = normal + rate * (target_ref[1] - normal) + SAG_FACTOR * emf * sine
        state_out_ref[0] = jnp.where(live, limit * jnp.tanh(new_axial / limit), axial)
        state_out_ref[1] = jnp.where(live, limit * jnp.tanh(new_normal / limit), normal)
        after = gcap * volts - hist_out_ref[...]
        hist_out_ref[...] = after
        put_state(after)
        return carry

    lax.fori_loop(0, STEPS, step, 0)
    cin[a, r] = current_ref[...] * (2.0 / STEPS)

    copies = []
    for d in range(1, group):
        block = cin.at[a, r]
        copy = send(block, block, rs.at[d], rr.at[d], (a, lax.rem(r + d, group)))
        copy.start()
        copies.append(copy)
    for copy in copies:
        copy.wait()
    copies = []
    for d in range(1, areas):
        block = cin.at[a]
        copy = send(block, block, cs.at[d], cr.at[d], (lax.rem(a + d, areas), r))
        copy.start()
        copies.append(copy)
    own_z.wait()
    for copy in z_copies:
        copy.wait()
    for copy in copies:
        copy.wait()
    members = group * ports
    for i in range(areas):
        for j in range(group):
            re, im = cin[i, j, 0], cin[i, j, 1]
            top = i * depth + j * ports
            flat_ref[top : top + ports, 0:128] = re
            flat_ref[top : top + ports, 128:256] = im
            flat_ref[top + members : top + members + ports, 0:128] = -im
            flat_ref[top + members : top + members + ports, 128:256] = re
    high, low = split(flat_ref[...])
    rh[...] = high
    rl[...] = low
    high, low = split(zin[...].reshape(areas * depth, chunk).T)
    total = mm(high, rh[...]) + mm(low, rh[...]) + mm(high, rl[...])
    mine[0] = total[:, 0:128]
    mine[1] = total[:, 128:256]

    inner = 2 ** ((areas.bit_length() - 1) // 2)
    outer = areas // inner
    zi = lax.div(a, inner)
    xi = lax.rem(a, inner)

    def region(part, who):
        return bus_ref.at[part, pl.ds(pl.multiple_of(who * chunk, 8), chunk), :]

    pending = []
    arrivals = []
    for part in range(2):
        local = pltpu.make_async_copy(mine.at[part], region(part, a), olocal.at[part])
        local.start()
        pending.append(local)
        for d in range(1, inner):
            to = zi * inner + lax.rem(xi + d, inner)
            k = part * areas + d
            copy = send(mine.at[part], region(part, a), os.at[k], orr.at[k], (to, r))
            copy.start()
            pending.append(copy)
        for d in range(1, outer):
            to = lax.rem(zi + d, outer) * inner + xi
            k = part * areas + inner * d
            copy = send(mine.at[part], region(part, a), os.at[k], orr.at[k], (to, r))
            copy.start()
            arrivals.append((part, d, copy))
    for part, d, copy in arrivals:
        copy.wait_recv()
        source = lax.rem(zi + outer - d, outer) * inner + xi
        for e in range(1, inner):
            to = zi * inner + lax.rem(xi + e, inner)
            k = part * areas + inner * d + e
            block = region(part, source)
            forward = send(block, block, fs.at[k], fr.at[k], (to, r))
            forward.start()
            pending.append(forward)
    for _, _, copy in arrivals:
        copy.wait_send()
    for copy in pending:
        copy.wait()


def vmem():
    return pl.BlockSpec(memory_space=pltpu.VMEM)


def smem():
    return pl.BlockSpec(memory_space=pltpu.SMEM)


def per_device(
    conductance_inverse,
    cap_history,
    cap_conductance,
    wave_history,
    line_partner,
    line_node,
    line_delay,
    line_admittance,
    conv_node,
    conv_count,
    conv_state,
    conv_reference,
    conv_rate,
    conv_limit,
    port_node,
    port_admittance,
    port_voltage_prev,
    port_bus,
    transfer_impedance,
):
    subnets = lax.axis_size(("area", "row"))
    own = lax.axis_index(("area", "row"))
    history = wave_history[0]
    lines = history.shape[1]
    half = lines // 2
    cases = history.shape[2]
    nodes = conductance_inverse.shape[1]
    convs = conv_node.shape[1]
    ports = port_node.shape[1]
    upper = history[:, :half]
    lower = history[:, half:]
    below1 = shifted(upper, 1)
    above1 = shifted(lower, -1)
    below2 = shifted(upper, 2)
    above2 = shifted(lower, -2)
    reach = (line_partner[0] - own) % subnets
    areas = lax.axis_size("area")
    group = lax.axis_size("row")
    bus_rows = transfer_impedance.shape[1]
    members = transfer_impedance.shape[2]
    chunk = bus_rows // areas
    zt = jnp.transpose(transfer_impedance, (0, 2, 1)).reshape(2 * members, bus_rows)
    zc = jnp.transpose(zt.reshape(2 * members, areas, chunk), (1, 0, 2))

    pad = 128 - lines - convs - ports
    index = jnp.concatenate([line_node, conv_node, port_node, jnp.full((1, pad), -1, jnp.int32)], axis=1)
    ones = jnp.ones((1, 128 - lines - convs), F32)
    coef = jnp.concatenate(
        [
            jnp.concatenate([2.0 * line_admittance, jnp.ones((1, convs), F32), port_admittance, ones[:, :pad]], axis=1),
            jnp.concatenate([jnp.ones((1, lines), F32), conv_rate, ones], axis=1),
            jnp.concatenate([jnp.ones((1, lines), F32), conv_limit, ones], axis=1),
        ],
        axis=0,
    )
    angles = jnp.arange(1, STEPS + 1, dtype=F32) * jnp.float32(2.0 * math.pi / STEPS)
    trig = jnp.stack([jnp.cos(angles), jnp.sin(angles)])
    flops = 2 * STEPS * (nodes + 128) * (2 * nodes + 256) * 256
    waves, hist_end, conv_out, _, bus_voltage = pl.pallas_call(
        functools.partial(window_kernel, lines, convs, ports),
        out_shape=(
            jax.ShapeDtypeStruct((STEPS, lines, cases), F32),
            jax.ShapeDtypeStruct((nodes, cases), F32),
            jax.ShapeDtypeStruct((2, convs, cases), F32),
            jax.ShapeDtypeStruct((areas * 2 * members, 2 * cases), F32),
            jax.ShapeDtypeStruct((2, bus_rows, cases), F32),
        ),
        in_specs=[smem()] * 4 + [vmem()] * 12 + [pl.BlockSpec(memory_space=pl.ANY)],
        out_specs=(vmem(),) * 4 + (pl.BlockSpec(memory_space=pl.ANY),),
        scratch_shapes=[
            pltpu.VMEM((nodes + 128, 2 * nodes + 256), BF16),
            pltpu.VMEM((nodes, 256), BF16),
            pltpu.VMEM((256, 256), BF16),
            pltpu.VMEM((128, nodes), F32),
            pltpu.VMEM((128, 128), F32),
            pltpu.VMEM((2, ports, cases), F32),
            pltpu.VMEM((areas, 2 * members, chunk), F32),
            pltpu.VMEM((areas, group, 2, ports, cases), F32),
            pltpu.VMEM((2, chunk, cases), F32),
            pltpu.VMEM((areas * 2 * members, 2 * cases), BF16),
            pltpu.VMEM((areas * 2 * members, 2 * cases), BF16),
            pltpu.SemaphoreType.DMA((areas,)),
            pltpu.SemaphoreType.DMA((areas,)),
            pltpu.SemaphoreType.DMA((group,)),
            pltpu.SemaphoreType.DMA((group,)),
            pltpu.SemaphoreType.DMA((areas,)),
            pltpu.SemaphoreType.DMA((areas,)),
            pltpu.SemaphoreType.DMA,
            pltpu.SemaphoreType.DMA((2 * areas,)),
            pltpu.SemaphoreType.DMA((2 * areas,)),
            pltpu.SemaphoreType.DMA((2 * areas,)),
            pltpu.SemaphoreType.DMA((2 * areas,)),
            pltpu.SemaphoreType.DMA((2,)),
        ],
        compiler_params=pltpu.CompilerParams(collective_id=0, has_side_effects=True),
        cost_estimate=pl.CostEstimate(flops=flops, bytes_accessed=8_000_000, transcendentals=0),
        name="window",
    )(
        reach,
        line_delay[0],
        trig,
        conv_count,
        index,
        coef,
        conductance_inverse[0],
        cap_conductance,
        cap_history[0],
        below1,
        below2,
        above1,
        above2,
        conv_state[0],
        conv_reference[0],
        port_voltage_prev[:, 0],
        zc,
    )

    local = port_bus.reshape(-1) - lax.axis_index("row") * bus_rows
    inside = (local >= 0) & (local < bus_rows)
    local = jnp.clip(local, 0, bus_rows - 1)
    chosen = jnp.concatenate([local, local + bus_rows])
    taken = jnp.take(bus_voltage.reshape(2 * bus_rows, cases), chosen, axis=0, mode="clip")
    taken = jnp.where(jnp.concatenate([inside, inside])[:, None], taken, 0.0)
    taken = taken.reshape(2, port_bus.shape[0], port_bus.shape[1], cases)
    port_voltage = lax.psum_scatter(taken, "row", scatter_dimension=1, tiled=True)
    return (waves[None], hist_end[None], conv_out[None], bus_voltage, port_voltage)


def solution(mesh):
    both = ("area", "row")
    placed = (
        P(both, None, None),
        P(both, None, None),
        P(both, None),
        P(both, None, None, None),
        P(both, None),
        P(both, None),
        P(both, None),
        P(both, None),
        P(both, None),
        P(both),
        P(both, None, None, None),
        P(both, None, None, None),
        P(both, None),
        P(both, None),
        P(both, None),
        P(both, None),
        P(None, both, None, None),
        P("area", None),
        P(None, "row", "area"),
    )
    return jax.shard_map(
        per_device,
        mesh=mesh,
        in_specs=placed,
        out_specs=(
            P(both, None, None, None),
            P(both, None, None),
            P(both, None, None, None),
            P(None, "row", None),
            P(None, both, None, None),
        ),
        check_vma=False,
    )
```
